32 devices in a mesh: parts: 2 (over x), row: 8 (over z, y), col: 2 (over core).
Axes of the slice: x: 2, y: 2, z: 4, core: 2. Of those that a mesh axis runs over, the one named last changes fastest.
Arguments:
- spectra: bfloat16 [4, 32, 2, 32, 1024], P('parts', None, None, ('row', 'col')), parts along dimension 0, may hold values from -6 to 6
- window_flags: int32 [64, 32], P('parts', ('row', 'col')), parts along dimension 0, may hold values 0 or 1
Outputs:
- cross: float32 [4, 2, 2, 16, 32, 1024], P('parts', None, 'col', None, 'row'), parts along dimension 0
The draws below stay inside these ranges and needn't reach their ends.
There are 2 independent parts, one for each index of `parts`. The reference program is written for one: setup_inputs(seed, part) draws one part's arguments, and reference() takes and returns one part's arrays. A program takes and returns all parts, laid end to end along the dimension named above; each array names one. Nothing has to cross between parts.
All inputs are finite; a program needn't handle non-finite values. No bound on the sum of `window_flags` on one device may be relied on, other than what follows from the above.
Results may differ from the reference program's by a relative error of at most 0.0034.
Values may be sent and summed in bfloat16 or wider, within the bound.
A program may use at most 256 MiB of HBM per device.

```python
import jax
import jax.numpy as jnp

CH_DEV = 2
W = 32
BANDS = 2
FB = 1024
HALFWIN = 64
C = 32
N_ROW = 8
N_COL = 2


def plant(entries, stream_key, least, largest):
    extent = entries.shape
    spot = [jax.random.randint(jax.random.fold_in(stream_key, axis), (), 0, extent[axis]) for axis in range(len(extent))]
    entries = entries.at[tuple(spot)].set(least)
    longest = extent.index(max(extent))
    spot[longest] = (spot[longest] + 1) % extent[longest]
    return entries.at[tuple(spot)].set(largest)


def block_levels(own_key, shape, cuts, least, top_value):
    gain, own = 1.0, jax.random.fold_in(own_key, 6)
    for axis_at, blocks in cuts:
        draws = jnp.exp(jax.random.uniform(jax.random.fold_in(own, axis_at), (blocks,), jnp.float32, least / len(cuts), top_value / len(cuts)))
        gain = gain * jnp.repeat(draws, shape[axis_at] // blocks).reshape([-1 if axis == axis_at else 1 for axis in range(len(shape))])
    return gain


def centred(key, extent, spread, bound, pieces=(), kind=jnp.bfloat16):
    drawn = jax.random.normal(key, extent, jnp.float32) * spread
    if len(pieces) > 0:
        drawn = block_levels(key, extent, pieces, -0.22, 0.18) * drawn
    return jnp.clip(drawn, min=-bound, max=bound).astype(kind)


def setup_inputs(seed: int = 0, part: int = 0) -> dict:
    key_of = jax.random.split(jax.random.key(seed), 3)
    own_keys = jax.random.split(jax.random.fold_in(key_of[2], part), 3)
    return {
        "spectra": centred(own_keys[0], (BANDS, W, 2, C, FB), 1.0, 6.0, ((3, 16),)),
        "window_flags": plant((jax.random.randint(own_keys[1], (W, C), 0, 4) < 3).astype(jnp.int32), jax.random.fold_in(own_keys[1], 1), 0, 1),
    }


epsilon = 1e-06

def window_mean(magnitude):
    bins = magnitude.shape[-1]
    lead = [(0, 0)] * (magnitude.ndim - 1)
    padded = jnp.pad(magnitude, lead + [(HALFWIN + 1, HALFWIN)])
    running = jnp.cumsum(padded, axis=-1)
    total = running[..., 2 * HALFWIN + 1:] - running[..., :bins]
    positions = jnp.arange(bins, dtype=jnp.int32)
    counted = (jnp.minimum(positions + HALFWIN, bins - 1) - jnp.maximum(positions - HALFWIN, 0) + 1).astype(jnp.float32)
    return total / counted

def whiten(values):
    magnitude = jnp.sqrt(values[:, :, 0] * values[:, :, 0] + values[:, :, 1] * values[:, :, 1])
    smooth = window_mean(magnitude)
    return (values / (smooth[:, :, None] + epsilon)).astype(jnp.bfloat16)

def reference(spectra, window_flags):
    flagged = spectra.astype(jnp.float32) * window_flags.astype(jnp.float32)[None, :, None, :, None]
    whitened = whiten(flagged)
    grouped = whitened.reshape(BANDS, W, 2, N_ROW, N_COL, CH_DEV, FB)
    total = N_ROW * N_COL * CH_DEV
    half_size = total // N_COL
    second = jnp.arange(total, dtype=jnp.int32)
    results = []
    for band_index in range(BANDS):
        halves = []
        for half_index in range(N_COL):
            first_rows = grouped[band_index, :, :, :, half_index].reshape(W, 2, half_size, FB).astype(jnp.float32)
            all_rows = whitened[band_index].astype(jnp.float32)
            prods = jnp.einsum('wpif,wqjf->pqijf', first_rows, all_rows)
            real_part = prods[0, 0] + prods[1, 1]
            imag_part = prods[1, 0] - prods[0, 1]
            slot = jnp.arange(half_size, dtype=jnp.int32)
            first = (slot // CH_DEV * N_COL + half_index) * CH_DEV + slot % CH_DEV
            keep = (first[:, None] <= second[None, :]).astype(jnp.float32)[:, :, None]
            halves.append(jnp.stack([real_part * keep, imag_part * keep], axis=0))
        results.append(jnp.stack(halves, axis=1))
    return jnp.stack(results, axis=0)
```

```python
import functools

import jax
import jax.numpy as jnp
from jax import lax
from jax.experimental import pallas as pl
from jax.experimental.pallas import tpu as pltpu
from jax.sharding import PartitionSpec as P

HALFWIN = 64
LANES = 128
epsilon = 1e-06


def window_mean(magnitude):
    bins = magnitude.shape[-1]
    lead = [(0, 0)] * (magnitude.ndim - 1)
    padded = jnp.pad(magnitude, lead + [(HALFWIN + 1, HALFWIN)])
    running = jnp.cumsum(padded, axis=-1)
    total = running[..., 2 * HALFWIN + 1 :] - running[..., :bins]
    positions = jnp.arange(bins, dtype=jnp.int32)
    counted = (
        jnp.minimum(positions + HALFWIN, bins - 1) - jnp.maximum(positions - HALFWIN, 0) + 1
    ).astype(jnp.float32)
    return total / counted


def whiten(values):
    magnitude = jnp.sqrt(values[:, :, 0] * values[:, :, 0] + values[:, :, 1] * values[:, :, 1])
    smooth = window_mean(magnitude)
    return (values / (smooth[:, :, None] + epsilon)).astype(jnp.bfloat16)


def combine_parts(prods, keep):
    real_part = prods[..., 0, 0, :, :, :] + prods[..., 1, 1, :, :, :]
    imag_part = prods[..., 1, 0, :, :, :] - prods[..., 0, 1, :, :, :]
    return jnp.stack([real_part * keep, imag_part * keep], axis=-4)


def gather_form(spectra, window_flags):
    per_device = spectra.shape[3]
    flag_values = window_flags.astype(jnp.float32)[None, :, None, :, None]
    payload = whiten(spectra.astype(jnp.float32) * flag_values)
    row_index = lax.axis_index("row")
    col_index = lax.axis_index("col")
    col_count = lax.axis_size("col")
    row_count = lax.axis_size("row")
    half_size = row_count * per_device
    cols_here = col_count * per_device
    slot = jnp.arange(half_size, dtype=jnp.int32)
    first = (slot // per_device * col_count + col_index) * per_device + slot % per_device
    second = row_index * cols_here + jnp.arange(cols_here, dtype=jnp.int32)
    keep = (first[:, None] <= second[None, :]).astype(jnp.float32)[:, :, None]
    pieces = []
    for band_index in range(spectra.shape[0]):
        first_rows = lax.all_gather(payload[band_index : band_index + 1], "row", axis=3, tiled=True)
        second_rows = lax.all_gather(
            payload[band_index : band_index + 1], "col", axis=3, tiled=True
        )
        prods = jnp.einsum(
            "wpif,wqjf->pqijf", first_rows[0], second_rows[0], preferred_element_type=jnp.float32
        )
        pieces.append(combine_parts(prods, keep))
    result = jnp.stack(pieces, axis=0)
    return result[:, :, None]


def whiten_kernel(x_ref, y_ref):
    bands, chans, _, windows, bins = x_ref.shape
    step = 2 * LANES
    chunks = bins // LANES
    near = lax.broadcasted_iota(jnp.int32, (2 * step, step), 0) - LANES
    here = lax.broadcasted_iota(jnp.int32, (2 * step, step), 1)
    inside = (jnp.abs(near - here) <= HALFWIN).astype(jnp.float32).astype(jnp.bfloat16)
    mags = []
    for b in range(bands):
        for c in range(chans):
            re = x_ref[b, c, 0].astype(jnp.float32)
            im = x_ref[b, c, 1].astype(jnp.float32)
            mags.append(jnp.sqrt(re * re + im * im))
    mag = jnp.concatenate(mags, axis=0)
    high = mag.astype(jnp.bfloat16)
    low = (mag - high.astype(jnp.float32)).astype(jnp.bfloat16)
    for at in range(0, bins, step):
        start, stop = max(at - LANES, 0), min(at + step + LANES, bins)
        near_rows = inside[start - at + LANES : stop - at + LANES]
        total = jnp.dot(
            high[:, start:stop], near_rows, preferred_element_type=jnp.float32
        ) + jnp.dot(low[:, start:stop], near_rows, preferred_element_type=jnp.float32)
        spot = at + lax.broadcasted_iota(jnp.int32, (1, step), 1)
        counted = (
            jnp.minimum(spot + HALFWIN, bins - 1) - jnp.maximum(spot - HALFWIN, 0) + 1
        ).astype(jnp.float32)
        scale = 1.0 / (total / counted + epsilon)
        for b in range(bands):
            for c in range(chans):
                top = (b * chans + c) * windows
                for p in range(2):
                    value = x_ref[b, c, p, :, at : at + step].astype(jnp.float32)
                    out = (value * scale[top : top + windows]).astype(jnp.bfloat16)
                    for half in range(2):
                        y_ref[
                            b * chunks + at // LANES + half,
                            pl.ds((c * 2 + p) * windows, windows),
                        ] = out[:, half * LANES : (half + 1) * LANES]


def exchange_kernel(count, cols, x_ref, y_ref, send_sem, recv_sem, own_sem):
    me = lax.axis_index("row") * cols + lax.axis_index("col")
    barrier = pltpu.get_barrier_semaphore()
    for k in range(1, count):
        peer = lax.rem(me + k, count)
        pl.semaphore_signal(
            barrier,
            inc=1,
            device_id={"row": peer // cols, "col": lax.rem(peer, cols)},
            device_id_type=pl.DeviceIdType.MESH,
        )
    own = pltpu.make_async_copy(x_ref.at[me], y_ref.at[me], own_sem)
    own.start()
    pl.semaphore_wait(barrier, count - 1)

    copies = []
    for k in range(1, count):
        peer = lax.rem(me + k, count)
        copy = pltpu.make_async_remote_copy(
            src_ref=x_ref.at[peer],
            dst_ref=y_ref.at[me],
            send_sem=send_sem.at[k],
            recv_sem=recv_sem.at[k],
            device_id={"row": peer // cols, "col": lax.rem(peer, cols)},
            device_id_type=pl.DeviceIdType.MESH,
        )
        copy.start()
        copies.append(copy)
    own.wait()
    for copy in copies:
        copy.wait()


def exchange(x, rows, cols, number):
    count = rows * cols
    return pl.pallas_call(
        functools.partial(exchange_kernel, count, cols),
        out_shape=jax.ShapeDtypeStruct(x.shape, x.dtype),
        in_specs=[pl.BlockSpec(memory_space=pl.ANY)],
        out_specs=pl.BlockSpec(memory_space=pl.ANY),
        scratch_shapes=[
            pltpu.SemaphoreType.DMA((count,)),
            pltpu.SemaphoreType.DMA((count,)),
            pltpu.SemaphoreType.DMA,
        ],
        compiler_params=pltpu.CompilerParams(collective_id=number, has_side_effects=True),
    )(x)


def fold(values):
    index = lax.broadcasted_iota(jnp.int32, values[0].shape, 0)
    shift = 1
    while len(values) > 1:
        even = lax.rem(index // shift, 2) == 0
        paired = []
        for n in range(0, len(values), 2):
            u, v = values[n], values[n + 1]
            moved = pltpu.roll(jnp.where(even, v, u), 8 - shift, 0)
            paired.append(jnp.where(even, u, v) + moved)
        values = paired
        shift *= 2
    return values[0]


def by_eight(values):
    total = values[0:8]
    for at in range(8, values.shape[0], 8):
        total = total + values[at : at + 8]
    return total


def cross_kernel(rows, cols, x_ref, o_ref, wide_ref):
    wide_ref[...] = x_ref[...].astype(jnp.float32)
    per_row = wide_ref.shape[0] // rows

    @pl.loop(0, rows)
    def _(r):
        @pl.loop(0, r + 1)
        def _(q):
            for h in range(cols):
                reals, imags = [], []
                for k in range(2):
                    first = q * per_row + h * 2 + k
                    re_a, im_a = wide_ref[first, 0], wide_ref[first, 1]
                    for n in range(per_row):
                        second = r * per_row + n
                        re_j, im_j = wide_ref[second, 0], wide_ref[second, 1]
                        reals.append(by_eight(re_a * re_j + im_a * im_j))
                        imags.append(by_eight(im_a * re_j - re_a * im_j))
                pair = jnp.concatenate([fold(reals), fold(imags)], axis=0)
                o_ref[r * cols + h, q] = pair.astype(jnp.bfloat16)

        @pl.loop(r + 1, rows)
        def _(q):
            for h in range(cols):
                o_ref[r * cols + h, q] = jnp.zeros(o_ref.shape[2:], jnp.bfloat16)


def place_kernel(bands, x_ref, o_ref):
    row, col = lax.axis_index("row"), lax.axis_index("col")
    chunks = x_ref.shape[0] // bands
    rows = x_ref.shape[1]
    index = lax.broadcasted_iota(jnp.int32, (8, LANES), 0)
    second = row * 4 + lax.rem(index, 4)
    for b in range(bands):
        for q in range(rows):
            first = q * 4 + col * 2 + index // 4
            keep = first <= second
            for c in range(chunks):
                pair = x_ref[b * chunks + c, q].astype(jnp.float32)
                for p in range(2):
                    value = jnp.where(keep, pair[p * 8 : p * 8 + 8], 0.0)
                    for k in range(2):
                        o_ref[b, p, 0, q * 2 + k, :, c * LANES : (c + 1) * LANES] = value[
                            k * 4 : k * 4 + 4
                        ]


def exchange_form(rows, cols, spectra, window_flags):
    bands, windows, parts, chans, bins = spectra.shape
    count = rows * cols
    flags = jnp.transpose(window_flags).astype(spectra.dtype)[None, :, None, :, None]
    values = jnp.transpose(spectra, (0, 3, 2, 1, 4)) * flags
    height = chans * parts * windows
    payload = pl.pallas_call(
        whiten_kernel,
        out_shape=jax.ShapeDtypeStruct((count, height, LANES), jnp.bfloat16),
    )(values)
    mine = exchange(payload, rows, cols, 0)
    mine = mine.reshape(count * chans, parts, windows, LANES)
    pairs = pl.pallas_call(
        functools.partial(cross_kernel, rows, cols),
        out_shape=jax.ShapeDtypeStruct((count, rows, 16, LANES), jnp.bfloat16),
        scratch_shapes=[pltpu.VMEM(mine.shape, jnp.float32)],
    )(mine)
    got = exchange(pairs, rows, cols, 1)
    return pl.pallas_call(
        functools.partial(place_kernel, bands),
        out_shape=jax.ShapeDtypeStruct((bands, 2, 1, rows * chans, cols * chans, bins), jnp.float32),
    )(got)


def solution(mesh):
    rows, cols = mesh.shape["row"], mesh.shape["col"]

    def on_device(spectra, window_flags):
        bands, windows, _, chans, bins = spectra.shape
        fits = (
            bands * bins == rows * cols * LANES
            and bins % (2 * LANES) == 0
            and chans == 2
            and cols == 2
            and windows % 16 == 0
        )
        if fits:
            return exchange_form(rows, cols, spectra, window_flags)
        return gather_form(spectra, window_flags)

    in_specs = (P("parts", None, None, ("row", "col"), None), P("parts", ("row", "col")))
    out_specs = P("parts", None, "col", None, "row", None)
    return jax.shard_map(
        on_device, mesh=mesh, in_specs=in_specs, out_specs=out_specs, check_vma=False
    )
```

```python
import functools

import jax
import jax.numpy as jnp
from jax import lax
from jax.experimental import pallas as pl
from jax.experimental.pallas import tpu as pltpu
from jax.sharding import PartitionSpec as P

HALFWIN = 64
LANES = 128
epsilon = 1e-06


def window_mean(magnitude):
    bins = magnitude.shape[-1]
    lead = [(0, 0)] * (magnitude.ndim - 1)
    padded = jnp.pad(magnitude, lead + [(HALFWIN + 1, HALFWIN)])
    running = jnp.cumsum(padded, axis=-1)
    total = running[..., 2 * HALFWIN + 1 :] - running[..., :bins]
    positions = jnp.arange(bins, dtype=jnp.int32)
    counted = (
        jnp.minimum(positions + HALFWIN, bins - 1) - jnp.maximum(positions - HALFWIN, 0) + 1
    ).astype(jnp.float32)
    return total / counted


def whiten(values):
    magnitude = jnp.sqrt(values[:, :, 0] * values[:, :, 0] + values[:, :, 1] * values[:, :, 1])
    smooth = window_mean(magnitude)
    return (values / (smooth[:, :, None] + epsilon)).astype(jnp.bfloat16)


def combine_parts(prods, keep):
    real_part = prods[..., 0, 0, :, :, :] + prods[..., 1, 1, :, :, :]
    imag_part = prods[..., 1, 0, :, :, :] - prods[..., 0, 1, :, :, :]
    return jnp.stack([real_part * keep, imag_part * keep], axis=-4)


def gather_form(spectra, window_flags):
    per_device = spectra.shape[3]
    flag_values = window_flags.astype(jnp.float32)[None, :, None, :, None]
    payload = whiten(spectra.astype(jnp.float32) * flag_values)
    row_index = lax.axis_index("row")
    col_index = lax.axis_index("col")
    col_count = lax.axis_size("col")
    row_count = lax.axis_size("row")
    half_size = row_count * per_device
    cols_here = col_count * per_device
    slot = jnp.arange(half_size, dtype=jnp.int32)
    first = (slot // per_device * col_count + col_index) * per_device + slot % per_device
    second = row_index * cols_here + jnp.arange(cols_here, dtype=jnp.int32)
    keep = (first[:, None] <= second[None, :]).astype(jnp.float32)[:, :, None]
    pieces = []
    for band_index in range(spectra.shape[0]):
        first_rows = lax.all_gather(payload[band_index : band_index + 1], "row", axis=3, tiled=True)
        second_rows = lax.all_gather(
            payload[band_index : band_index + 1], "col", axis=3, tiled=True
        )
        prods = jnp.einsum(
            "wpif,wqjf->pqijf", first_rows[0], second_rows[0], preferred_element_type=jnp.float32
        )
        pieces.append(combine_parts(prods, keep))
    result = jnp.stack(pieces, axis=0)
    return result[:, :, None]


def whiten_windows(x_ref, y_ref, start_window, count_windows):
    bands, chans, _, _, bins = x_ref.shape
    step = 2 * LANES
    chunks = bins // LANES
    near = lax.broadcasted_iota(jnp.int32, (2 * step, step), 0) - LANES
    here = lax.broadcasted_iota(jnp.int32, (2 * step, step), 1)
    inside = (jnp.abs(near - here) <= HALFWIN).astype(jnp.float32).astype(jnp.bfloat16)
    picked = pl.ds(start_window, count_windows)
    mags = []
    for b in range(bands):
        for c in range(chans):
            re = x_ref[b, c, 0, picked].astype(jnp.float32)
            im = x_ref[b, c, 1, picked].astype(jnp.float32)
            mags.append(jnp.sqrt(re * re + im * im))
    mag = jnp.concatenate(mags, axis=0)
    high = mag.astype(jnp.bfloat16)
    low = (mag - high.astype(jnp.float32)).astype(jnp.bfloat16)
    for at in range(0, bins, step):
        start, stop = max(at - LANES, 0), min(at + step + LANES, bins)
        near_rows = inside[start - at + LANES : stop - at + LANES]
        total = jnp.dot(
            high[:, start:stop], near_rows, preferred_element_type=jnp.float32
        ) + jnp.dot(low[:, start:stop], near_rows, preferred_element_type=jnp.float32)
        spot = at + lax.broadcasted_iota(jnp.int32, (1, step), 1)
        counted = (
            jnp.minimum(spot + HALFWIN, bins - 1) - jnp.maximum(spot - HALFWIN, 0) + 1
        ).astype(jnp.float32)
        scale = 1.0 / (total / counted + epsilon)
        for b in range(bands):
            for c in range(chans):
                top = (b * chans + c) * count_windows
                for p in range(2):
                    value = x_ref[b, c, p, picked, at : at + step].astype(jnp.float32)
                    out = (value * scale[top : top + count_windows]).astype(jnp.bfloat16)
                    for half in range(2):
                        y_ref[
                            b * chunks + at // LANES + half,
                            pl.ds((c * 2 + p) * count_windows, count_windows),
                        ] = out[:, half * LANES : (half + 1) * LANES]


def fold(values):
    index = lax.broadcasted_iota(jnp.int32, values[0].shape, 0)
    shift = 1
    while len(values) > 1:
        even = lax.rem(index // shift, 2) == 0
        paired = []
        for n in range(0, len(values), 2):
            u, v = values[n], values[n + 1]
            moved = pltpu.roll(jnp.where(even, v, u), 8 - shift, 0)
            paired.append(jnp.where(even, u, v) + moved)
        values = paired
        shift *= 2
    return values[0]


def by_eight(values):
    total = values[0:8]
    for at in range(8, values.shape[0], 8):
        total = total + values[at : at + 8]
    return total


def cross_row(wide_ref, r, rows, cols, finish):
    per_row = wide_ref.shape[0] // rows

    @pl.loop(0, r + 1)
    def _(q):
        for h in range(cols):
            reals, imags = [], []
            for k in range(2):
                first = q * per_row + h * 2 + k
                re_a, im_a = wide_ref[first, 0], wide_ref[first, 1]
                for n in range(per_row):
                    second = r * per_row + n
                    re_j, im_j = wide_ref[second, 0], wide_ref[second, 1]
                    reals.append(by_eight(re_a * re_j + im_a * im_j))
                    imags.append(by_eight(im_a * re_j - re_a * im_j))
            finish(h, q, jnp.concatenate([fold(reals), fold(imags)], axis=0))


def main_kernel(
    rows, cols, x_ref, got_ref, sent, held, wide_ref, total_ref, pairs,
    send_sem, recv_sem, own_sem, back_send, back_recv, back_own,
):
    count = rows * cols
    windows = x_ref.shape[3]
    part_windows = windows // 2
    row, col = lax.axis_index("row"), lax.axis_index("col")
    me = row * cols + col
    order = sorted(range(1, count), key=lambda k: abs(k - count // 2))

    def place_of(peer):
        return {"row": peer // cols, "col": lax.rem(peer, cols)}

    barrier = pltpu.get_barrier_semaphore()
    for k in range(1, count):
        pl.semaphore_signal(
            barrier,
            inc=1,
            device_id=place_of(lax.rem(me + k, count)),
            device_id_type=pl.DeviceIdType.MESH,
        )
    copies, owns = [[], []], []
    for half in range(2):
        whiten_windows(x_ref, sent.at[half], half * part_windows, part_windows)
        if half == 0:
            pl.semaphore_wait(barrier, count - 1)
        for k in order:
            peer = lax.rem(me + k, count)
            copy = pltpu.make_async_remote_copy(
                src_ref=sent.at[half, peer],
                dst_ref=held.at[half, me],
                send_sem=send_sem.at[half, k],
                recv_sem=recv_sem.at[half, k],
                device_id=place_of(peer),
                device_id_type=pl.DeviceIdType.MESH,
            )
            copy.start()
            copies[half].append(copy)
        own = pltpu.make_async_copy(sent.at[half, me], held.at[half, me], own_sem.at[half])
        own.start()
        owns.append(own)

    def widen(half):
        owns[half].wait()
        for copy in copies[half]:
            copy.wait_recv()

        @pl.loop(0, count)
        def _(n):
            for c in range(2):
                for p in range(2):
                    wide_ref[n * 2 + c, p] = held[
                        half, n, pl.ds((c * 2 + p) * part_windows, part_windows)
                    ].astype(jnp.float32)

    widen(0)

    @pl.loop(0, rows)
    def _(r):
        def keep(h, q, value):
            total_ref[r * cols + h, q] = value

        cross_row(wide_ref, r, rows, cols, keep)

    widen(1)

    def back_copy(k, h):
        to = k * cols + h
        return pltpu.make_async_remote_copy(
            src_ref=pairs.at[to, pl.ds(0, k + 1)],
            dst_ref=got_ref.at[me, pl.ds(0, k + 1)],
            send_sem=back_send.at[to],
            recv_sem=back_recv.at[me],
            device_id={"row": k, "col": h},
            device_id_type=pl.DeviceIdType.MESH,
        )

    def own_copy(k, h):
        to = k * cols + h
        return pltpu.make_async_copy(
            pairs.at[to, pl.ds(0, k + 1)], got_ref.at[to, pl.ds(0, k + 1)], back_own
        )

    @pl.loop(0, rows)
    def _(step):
        r = lax.rem(row + rows // 2 + step, rows)

        def keep(h, q, value):
            pairs[r * cols + h, q] = (total_ref[r * cols + h, q] + value).astype(jnp.bfloat16)

        cross_row(wide_ref, r, rows, cols, keep)
        for k in range(rows):

            @pl.when(r == k)
            def _():
                for h in range(cols):

                    @pl.when(me != k * cols + h)
                    def _():
                        back_copy(k, h).start()

                    @pl.when(me == k * cols + h)
                    def _():
                        own_copy(k, h).start()

    for half in range(2):
        for copy in copies[half]:
            copy.wait_send()
    for k in range(rows):
        for h in range(cols):

            @pl.when(me != k * cols + h)
            def _():
                back_copy(k, h).wait_send()

    for k in range(rows):

        @pl.when(row == k)
        def _():
            for n in range(count):

                @pl.when(me != n)
                def _():
                    pltpu.make_async_remote_copy(
                        src_ref=pairs.at[0, pl.ds(0, k + 1)],
                        dst_ref=got_ref.at[n, pl.ds(0, k + 1)],
                        send_sem=back_send.at[n],
                        recv_sem=back_recv.at[n],
                        device_id={"row": n // cols, "col": n % cols},
                        device_id_type=pl.DeviceIdType.MESH,
                    ).wait_recv()

                @pl.when(me == n)
                def _():
                    own_copy(k, n % cols).wait()


def place_kernel(bands, x_ref, o_ref):
    row, col = lax.axis_index("row"), lax.axis_index("col")
    chunks = x_ref.shape[0] // bands
    rows = x_ref.shape[1]
    index = lax.broadcasted_iota(jnp.int32, (8, LANES), 0)
    second = row * 4 + lax.rem(index, 4)
    for b in range(bands):
        for q in range(rows):
            first = q * 4 + col * 2 + index // 4
            keep = first <= second
            for c in range(chunks):
                pair = x_ref[b * chunks + c, q].astype(jnp.float32)
                for p in range(2):
                    value = jnp.where(keep, pair[p * 8 : p * 8 + 8], 0.0)
                    for k in range(2):
                        o_ref[b, p, 0, q * 2 + k, :, c * LANES : (c + 1) * LANES] = value[
                            k * 4 : k * 4 + 4
                        ]


def exchange_form(rows, cols, spectra, window_flags):
    bands, windows, parts, chans, bins = spectra.shape
    count = rows * cols
    flags = jnp.transpose(window_flags).astype(spectra.dtype)[None, :, None, :, None]
    values = jnp.transpose(spectra, (0, 3, 2, 1, 4)) * flags
    height = chans * parts * windows
    got = pl.pallas_call(
        functools.partial(main_kernel, rows, cols),
        out_shape=jax.ShapeDtypeStruct((count, rows, 16, LANES), jnp.bfloat16),
        in_specs=[pl.BlockSpec(memory_space=pltpu.VMEM)],
        out_specs=pl.BlockSpec(memory_space=pl.ANY),
        scratch_shapes=[
            pltpu.VMEM((2, count, height // 2, LANES), jnp.bfloat16),
            pltpu.VMEM((2, count, height // 2, LANES), jnp.bfloat16),
            pltpu.VMEM((count * chans, parts, windows // 2, LANES), jnp.float32),
            pltpu.VMEM((count, rows, 16, LANES), jnp.float32),
            pltpu.VMEM((count, rows, 16, LANES), jnp.bfloat16),
            pltpu.SemaphoreType.DMA((2, count)),
            pltpu.SemaphoreType.DMA((2, count)),
            pltpu.SemaphoreType.DMA((2,)),
            pltpu.SemaphoreType.DMA((count,)),
            pltpu.SemaphoreType.DMA((count,)),
            pltpu.SemaphoreType.DMA,
        ],
        compiler_params=pltpu.CompilerParams(collective_id=0, has_side_effects=True),
    )(values)
    return pl.pallas_call(
        functools.partial(place_kernel, bands),
        out_shape=jax.ShapeDtypeStruct((bands, 2, 1, rows * chans, cols * chans, bins), jnp.float32),
    )(got)


def solution(mesh):
    rows, cols = mesh.shape["row"], mesh.shape["col"]

    def on_device(spectra, window_flags):
        bands, windows, _, chans, bins = spectra.shape
        fits = (
            bands * bins == rows * cols * LANES
            and bins % (2 * LANES) == 0
            and chans == 2
            and cols == 2
            and windows % 32 == 0
        )
        if fits:
            return exchange_form(rows, cols, spectra, window_flags)
        return gather_form(spectra, window_flags)

    in_specs = (P("parts", None, None, ("row", "col"), None), P("parts", ("row", "col")))
    out_specs = P("parts", None, "col", None, "row", None)
    return jax.shard_map(
        on_device, mesh=mesh, in_specs=in_specs, out_specs=out_specs, check_vma=False
    )
```

```python
import functools

import jax
import jax.numpy as jnp
from jax import lax
from jax.experimental import pallas as pl
from jax.experimental.pallas import tpu as pltpu
from jax.sharding import PartitionSpec as P

HALFWIN = 64
LANES = 128
epsilon = 1e-06


def window_mean(magnitude):
    bins = magnitude.shape[-1]
    lead = [(0, 0)] * (magnitude.ndim - 1)
    padded = jnp.pad(magnitude, lead + [(HALFWIN + 1, HALFWIN)])
    running = jnp.cumsum(padded, axis=-1)
    total = running[..., 2 * HALFWIN + 1 :] - running[..., :bins]
    positions = jnp.arange(bins, dtype=jnp.int32)
    counted = (
        jnp.minimum(positions + HALFWIN, bins - 1) - jnp.maximum(positions - HALFWIN, 0) + 1
    ).astype(jnp.float32)
    return total / counted


def whiten(values):
    magnitude = jnp.sqrt(values[:, :, 0] * values[:, :, 0] + values[:, :, 1] * values[:, :, 1])
    smooth = window_mean(magnitude)
    return (values / (smooth[:, :, None] + epsilon)).astype(jnp.bfloat16)


def combine_parts(prods, keep):
    real_part = prods[..., 0, 0, :, :, :] + prods[..., 1, 1, :, :, :]
    imag_part = prods[..., 1, 0, :, :, :] - prods[..., 0, 1, :, :, :]
    return jnp.stack([real_part * keep, imag_part * keep], axis=-4)


def gather_form(spectra, window_flags):
    per_device = spectra.shape[3]
    flag_values = window_flags.astype(jnp.float32)[None, :, None, :, None]
    payload = whiten(spectra.astype(jnp.float32) * flag_values)
    row_index = lax.axis_index("row")
    col_index = lax.axis_index("col")
    col_count = lax.axis_size("col")
    row_count = lax.axis_size("row")
    half_size = row_count * per_device
    cols_here = col_count * per_device
    slot = jnp.arange(half_size, dtype=jnp.int32)
    first = (slot // per_device * col_count + col_index) * per_device + slot % per_device
    second = row_index * cols_here + jnp.arange(cols_here, dtype=jnp.int32)
    keep = (first[:, None] <= second[None, :]).astype(jnp.float32)[:, :, None]
    pieces = []
    for band_index in range(spectra.shape[0]):
        first_rows = lax.all_gather(payload[band_index : band_index + 1], "row", axis=3, tiled=True)
        second_rows = lax.all_gather(
            payload[band_index : band_index + 1], "col", axis=3, tiled=True
        )
        prods = jnp.einsum(
            "wpif,wqjf->pqijf", first_rows[0], second_rows[0], preferred_element_type=jnp.float32
        )
        pieces.append(combine_parts(prods, keep))
    result = jnp.stack(pieces, axis=0)
    return result[:, :, None]


def spread_windows(x_ref, flag_ref, rows_ref, start_window, count_windows):
    bands, _, parts, chans, _ = x_ref.shape
    for b in range(bands):
        for w in range(count_windows):
            for p in range(parts):
                pair = x_ref[b, start_window + w, p].astype(jnp.float32)
                for n in range(rows_ref.shape[2]):
                    rows_ref[b, p, n, pl.ds(w * chans, chans)] = pair[:, n * LANES : (n + 1) * LANES]
    extent = (count_windows, flag_ref.shape[1])
    here = lax.broadcasted_iota(jnp.int32, extent, 0) + start_window
    same = here == lax.broadcasted_iota(jnp.int32, extent, 1)
    flags = flag_ref[...].astype(jnp.float32)
    return [
        jnp.sum(jnp.where(same, flags[c : c + 1], 0.0), axis=1, keepdims=True)
        for c in range(chans)
    ]


def whiten_windows(x_ref, flag_ref, rows_ref, y_ref, start_window, count_windows):
    bands, _, _, chans, bins = x_ref.shape
    flags = spread_windows(x_ref, flag_ref, rows_ref, start_window, count_windows)
    step = 2 * LANES
    chunks = bins // LANES
    near = lax.broadcasted_iota(jnp.int32, (2 * step, step), 0) - LANES
    here = lax.broadcasted_iota(jnp.int32, (2 * step, step), 1)
    inside = (jnp.abs(near - here) <= HALFWIN).astype(jnp.float32).astype(jnp.bfloat16)
    mags = []
    for b in range(bands):
        for c in range(chans):
            picked = pl.ds(c, count_windows, stride=chans)
            line = []
            for n in range(chunks):
                re = rows_ref[b, 0, n, picked] * flags[c]
                im = rows_ref[b, 1, n, picked] * flags[c]
                line.append(jnp.sqrt(re * re + im * im))
            mags.append(jnp.concatenate(line, axis=1))
    mag = jnp.concatenate(mags, axis=0)
    high = mag.astype(jnp.bfloat16)
    low = (mag - high.astype(jnp.float32)).astype(jnp.bfloat16)
    for at in range(0, bins, step):
        start, stop = max(at - LANES, 0), min(at + step + LANES, bins)
        near_rows = inside[start - at + LANES : stop - at + LANES]
        total = jnp.dot(
            high[:, start:stop], near_rows, preferred_element_type=jnp.float32
        ) + jnp.dot(low[:, start:stop], near_rows, preferred_element_type=jnp.float32)
        spot = at + lax.broadcasted_iota(jnp.int32, (1, step), 1)
        counted = (
            jnp.minimum(spot + HALFWIN, bins - 1) - jnp.maximum(spot - HALFWIN, 0) + 1
        ).astype(jnp.float32)
        scale = 1.0 / (total / counted + epsilon)
        for b in range(bands):
            for c in range(chans):
                top = (b * chans + c) * count_windows
                picked = pl.ds(c, count_windows, stride=chans)
                for p in range(2):
                    for half in range(2):
                        lanes = slice(half * LANES, (half + 1) * LANES)
                        value = rows_ref[b, p, at // LANES + half, picked] * flags[c]
                        out = value * scale[top : top + count_windows, lanes]
                        y_ref[
                            b * chunks + at // LANES + half,
                            pl.ds((c * 2 + p) * count_windows, count_windows),
                        ] = out.astype(jnp.bfloat16)


def fold(values):
    index = lax.broadcasted_iota(jnp.int32, values[0].shape, 0)
    shift = 1
    while len(values) > 1:
        even = lax.rem(index // shift, 2) == 0
        paired = []
        for n in range(0, len(values), 2):
            u, v = values[n], values[n + 1]
            moved = pltpu.roll(jnp.where(even, v, u), 8 - shift, 0)
            paired.append(jnp.where(even, u, v) + moved)
        values = paired
        shift *= 2
    return values[0]


def by_eight(values):
    total = values[0:8]
    for at in range(8, values.shape[0], 8):
        total = total + values[at : at + 8]
    return total


def cross_row(wide_ref, r, rows, cols, finish):
    per_row = wide_ref.shape[0] // rows

    @pl.loop(0, r + 1)
    def _(q):
        for h in range(cols):
            reals, imags = [], []
            for k in range(2):
                first = q * per_row + h * 2 + k
                re_a, im_a = wide_ref[first, 0], wide_ref[first, 1]
                for n in range(per_row):
                    second = r * per_row + n
                    re_j, im_j = wide_ref[second, 0], wide_ref[second, 1]
                    reals.append(by_eight(re_a * re_j + im_a * im_j))
                    imags.append(by_eight(im_a * re_j - re_a * im_j))
            finish(h, q, jnp.concatenate([fold(reals), fold(imags)], axis=0))


def main_kernel(
    rows, cols, x_ref, flag_ref, got_ref, spread, sent, held, wide_ref, total_ref, pairs,
    send_sem, recv_sem, own_sem, back_send, back_recv, back_own,
):
    count = rows * cols
    windows = x_ref.shape[1]
    part_windows = windows // 2
    row, col = lax.axis_index("row"), lax.axis_index("col")
    me = row * cols + col
    order = sorted(range(1, count), key=lambda k: abs(k - count // 2))

    def place_of(peer):
        return {"row": peer // cols, "col": lax.rem(peer, cols)}

    barrier = pltpu.get_barrier_semaphore()
    for k in range(1, count):
        pl.semaphore_signal(
            barrier,
            inc=1,
            device_id=place_of(lax.rem(me + k, count)),
            device_id_type=pl.DeviceIdType.MESH,
        )
    copies, owns = [[], []], []
    for half in range(2):
        whiten_windows(x_ref, flag_ref, spread, sent.at[half], half * part_windows, part_windows)
        if half == 0:
            pl.semaphore_wait(barrier, count - 1)
        for k in order:
            peer = lax.rem(me + k, count)
            copy = pltpu.make_async_remote_copy(
                src_ref=sent.at[half, peer],
                dst_ref=held.at[half, me],
                send_sem=send_sem.at[half, k],
                recv_sem=recv_sem.at[half, k],
                device_id=place_of(peer),
                device_id_type=pl.DeviceIdType.MESH,
            )
            copy.start()
            copies[half].append(copy)
        own = pltpu.make_async_copy(sent.at[half, me], held.at[half, me], own_sem.at[half])
        own.start()
        owns.append(own)

    def widen(half):
        owns[half].wait()
        for copy in copies[half]:
            copy.wait_recv()

        @pl.loop(0, count)
        def _(n):
            for c in range(2):
                for p in range(2):
                    wide_ref[n * 2 + c, p] = held[
                        half, n, pl.ds((c * 2 + p) * part_windows, part_windows)
                    ].astype(jnp.float32)

    widen(0)

    @pl.loop(0, rows)
    def _(r):
        def keep(h, q, value):
            total_ref[r * cols + h, q] = value

        cross_row(wide_ref, r, rows, cols, keep)

    widen(1)

    def back_copy(k, h):
        to = k * cols + h
        return pltpu.make_async_remote_copy(
            src_ref=pairs.at[to, pl.ds(0, k + 1)],
            dst_ref=got_ref.at[me, pl.ds(0, k + 1)],
            send_sem=back_send.at[to],
            recv_sem=back_recv.at[me],
            device_id={"row": k, "col": h},
            device_id_type=pl.DeviceIdType.MESH,
        )

    def own_copy(k, h):
        to = k * cols + h
        return pltpu.make_async_copy(
            pairs.at[to, pl.ds(0, k + 1)], got_ref.at[to, pl.ds(0, k + 1)], back_own
        )

    @pl.loop(0, rows)
    def _(step):
        r = lax.rem(row + rows // 2 + step, rows)

        def keep(h, q, value):
            pairs[r * cols + h, q] = (total_ref[r * cols + h, q] + value).astype(jnp.bfloat16)

        cross_row(wide_ref, r, rows, cols, keep)
        for k in range(rows):

            @pl.when(r == k)
            def _():
                for h in range(cols):

                    @pl.when(me != k * cols + h)
                    def _():
                        back_copy(k, h).start()

                    @pl.when(me == k * cols + h)
                    def _():
                        own_copy(k, h).start()

    for half in range(2):
        for copy in copies[half]:
            copy.wait_send()
    for k in range(rows):
        for h in range(cols):

            @pl.when(me != k * cols + h)
            def _():
                back_copy(k, h).wait_send()

    for k in range(rows):

        @pl.when(row == k)
        def _():
            for n in range(count):

                @pl.when(me != n)
                def _():
                    pltpu.make_async_remote_copy(
                        src_ref=pairs.at[0, pl.ds(0, k + 1)],
                        dst_ref=got_ref.at[n, pl.ds(0, k + 1)],
                        send_sem=back_send.at[n],
                        recv_sem=back_recv.at[n],
                        device_id={"row": n // cols, "col": n % cols},
                        device_id_type=pl.DeviceIdType.MESH,
                    ).wait_recv()

                @pl.when(me == n)
                def _():
                    own_copy(k, n % cols).wait()


def place_kernel(x_ref, o_ref):
    row, col = lax.axis_index("row"), lax.axis_index("col")
    chunks, rows = x_ref.shape[:2]
    index = lax.broadcasted_iota(jnp.int32, (8, LANES), 0)
    second = row * 4 + lax.rem(index, 4)
    for q in range(rows):
        keep = q * 4 + col * 2 + index // 4 <= second
        for c in range(chunks):
            pair = x_ref[c, q].astype(jnp.float32)
            for p in range(2):
                value = jnp.where(keep, pair[p * 8 : p * 8 + 8], 0.0)
                for k in range(2):
                    o_ref[0, p, 0, q * 2 + k, :, c * LANES : (c + 1) * LANES] = value[
                        k * 4 : k * 4 + 4
                    ]


def exchange_form(rows, cols, spectra, window_flags):
    bands, windows, parts, chans, bins = spectra.shape
    count = rows * cols
    height = chans * parts * windows
    got = pl.pallas_call(
        functools.partial(main_kernel, rows, cols),
        out_shape=jax.ShapeDtypeStruct((count, rows, 16, LANES), jnp.bfloat16),
        in_specs=[pl.BlockSpec(memory_space=pltpu.VMEM)] * 2,
        out_specs=pl.BlockSpec(memory_space=pl.ANY),
        scratch_shapes=[
            pltpu.VMEM((bands, parts, bins // LANES, windows // 2 * chans, LANES), jnp.float32),
            pltpu.VMEM((2, count, height // 2, LANES), jnp.bfloat16),
            pltpu.VMEM((2, count, height // 2, LANES), jnp.bfloat16),
            pltpu.VMEM((count * chans, parts, windows // 2, LANES), jnp.float32),
            pltpu.VMEM((count, rows, 16, LANES), jnp.float32),
            pltpu.VMEM((count, rows, 16, LANES), jnp.bfloat16),
            pltpu.SemaphoreType.DMA((2, count)),
            pltpu.SemaphoreType.DMA((2, count)),
            pltpu.SemaphoreType.DMA((2,)),
            pltpu.SemaphoreType.DMA((count,)),
            pltpu.SemaphoreType.DMA((count,)),
            pltpu.SemaphoreType.DMA,
        ],
        compiler_params=pltpu.CompilerParams(collective_id=0, has_side_effects=True),
    )(spectra, jnp.transpose(window_flags))
    chunks = count // bands // 2
    return pl.pallas_call(
        place_kernel,
        grid=(bands, 2),
        in_specs=[pl.BlockSpec((chunks, rows, 16, LANES), lambda b, n: (b * 2 + n, 0, 0, 0))],
        out_specs=pl.BlockSpec(
            (1, 2, 1, rows * chans, cols * chans, bins // 2), lambda b, n: (b, 0, 0, 0, 0, n)
        ),
        out_shape=jax.ShapeDtypeStruct((bands, 2, 1, rows * chans, cols * chans, bins), jnp.float32),
    )(got)


def solution(mesh):
    rows, cols = mesh.shape["row"], mesh.shape["col"]

    def on_device(spectra, window_flags):
        bands, windows, _, chans, bins = spectra.shape
        fits = (
            bands * bins == rows * cols * LANES
            and bins % (2 * LANES) == 0
            and chans == 2
            and cols == 2
            and windows % 32 == 0
        )
        if fits:
            return exchange_form(rows, cols, spectra, window_flags)
        return gather_form(spectra, window_flags)

    in_specs = (P("parts", None, None, ("row", "col"), None), P("parts", ("row", "col")))
    out_specs = P("parts", None, "col", None, "row", None)
    return jax.shard_map(
        on_device, mesh=mesh, in_specs=in_specs, out_specs=out_specs, check_vma=False
    )
```

```python
import functools

import jax
import jax.numpy as jnp
from jax import lax
from jax.experimental import pallas as pl
from jax.experimental.pallas import tpu as pltpu
from jax.sharding import PartitionSpec as P

HALFWIN = 64
LANES = 128
epsilon = 1e-06


def window_mean(magnitude):
    bins = magnitude.shape[-1]
    lead = [(0, 0)] * (magnitude.ndim - 1)
    padded = jnp.pad(magnitude, lead + [(HALFWIN + 1, HALFWIN)])
    running = jnp.cumsum(padded, axis=-1)
    total = running[..., 2 * HALFWIN + 1 :] - running[..., :bins]
    positions = jnp.arange(bins, dtype=jnp.int32)
    counted = (
        jnp.minimum(positions + HALFWIN, bins - 1) - jnp.maximum(positions - HALFWIN, 0) + 1
    ).astype(jnp.float32)
    return total / counted


def whiten(values):
    magnitude = jnp.sqrt(values[:, :, 0] * values[:, :, 0] + values[:, :, 1] * values[:, :, 1])
    smooth = window_mean(magnitude)
    return (values / (smooth[:, :, None] + epsilon)).astype(jnp.bfloat16)


def combine_parts(prods, keep):
    real_part = prods[..., 0, 0, :, :, :] + prods[..., 1, 1, :, :, :]
    imag_part = prods[..., 1, 0, :, :, :] - prods[..., 0, 1, :, :, :]
    return jnp.stack([real_part * keep, imag_part * keep], axis=-4)


def gather_form(spectra, window_flags):
    per_device = spectra.shape[3]
    flag_values = window_flags.astype(jnp.float32)[None, :, None, :, None]
    payload = whiten(spectra.astype(jnp.float32) * flag_values)
    row_index = lax.axis_index("row")
    col_index = lax.axis_index("col")
    col_count = lax.axis_size("col")
    row_count = lax.axis_size("row")
    half_size = row_count * per_device
    cols_here = col_count * per_device
    slot = jnp.arange(half_size, dtype=jnp.int32)
    first = (slot // per_device * col_count + col_index) * per_device + slot % per_device
    second = row_index * cols_here + jnp.arange(cols_here, dtype=jnp.int32)
    keep = (first[:, None] <= second[None, :]).astype(jnp.float32)[:, :, None]
    pieces = []
    for band_index in range(spectra.shape[0]):
        first_rows = lax.all_gather(payload[band_index : band_index + 1], "row", axis=3, tiled=True)
        second_rows = lax.all_gather(
            payload[band_index : band_index + 1], "col", axis=3, tiled=True
        )
        prods = jnp.einsum(
            "wpif,wqjf->pqijf", first_rows[0], second_rows[0], preferred_element_type=jnp.float32
        )
        pieces.append(combine_parts(prods, keep))
    result = jnp.stack(pieces, axis=0)
    return result[:, :, None]


def spread_windows(x_ref, flag_ref, rows_ref, start_window, count_windows):
    bands, _, parts, chans, _ = x_ref.shape
    for b in range(bands):
        for w in range(count_windows):
            for p in range(parts):
                pair = x_ref[b, start_window + w, p].astype(jnp.float32)
                for n in range(rows_ref.shape[2]):
                    rows_ref[b, p, n, pl.ds(w * chans, chans)] = pair[:, n * LANES : (n + 1) * LANES]
    extent = (count_windows, flag_ref.shape[1])
    here = lax.broadcasted_iota(jnp.int32, extent, 0) + start_window
    same = here == lax.broadcasted_iota(jnp.int32, extent, 1)
    flags = flag_ref[...].astype(jnp.float32)
    return [
        jnp.sum(jnp.where(same, flags[c : c + 1], 0.0), axis=1, keepdims=True)
        for c in range(chans)
    ]


def whiten_windows(x_ref, flag_ref, rows_ref, y_ref, start_window, count_windows):
    bands, _, _, chans, bins = x_ref.shape
    flags = spread_windows(x_ref, flag_ref, rows_ref, start_window, count_windows)
    step = 2 * LANES
    chunks = bins // LANES
    near = lax.broadcasted_iota(jnp.int32, (2 * step, step), 0) - LANES
    here = lax.broadcasted_iota(jnp.int32, (2 * step, step), 1)
    inside = (jnp.abs(near - here) <= HALFWIN).astype(jnp.float32).astype(jnp.bfloat16)
    mags = []
    for b in range(bands):
        for c in range(chans):
            picked = pl.ds(c, count_windows, stride=chans)
            line = []
            for n in range(chunks):
                re = rows_ref[b, 0, n, picked] * flags[c]
                im = rows_ref[b, 1, n, picked] * flags[c]
                line.append(jnp.sqrt(re * re + im * im))
            mags.append(jnp.concatenate(line, axis=1))
    mag = jnp.concatenate(mags, axis=0)
    high = mag.astype(jnp.bfloat16)
    low = (mag - high.astype(jnp.float32)).astype(jnp.bfloat16)
    for at in range(0, bins, step):
        start, stop = max(at - LANES, 0), min(at + step + LANES, bins)
        near_rows = inside[start - at + LANES : stop - at + LANES]
        total = jnp.dot(
            high[:, start:stop], near_rows, preferred_element_type=jnp.float32
        ) + jnp.dot(low[:, start:stop], near_rows, preferred_element_type=jnp.float32)
        spot = at + lax.broadcasted_iota(jnp.int32, (1, step), 1)
        counted = (
            jnp.minimum(spot + HALFWIN, bins - 1) - jnp.maximum(spot - HALFWIN, 0) + 1
        ).astype(jnp.float32)
        scale = 1.0 / (total / counted + epsilon)
        for b in range(bands):
            for c in range(chans):
                top = (b * chans + c) * count_windows
                picked = pl.ds(c, count_windows, stride=chans)
                for p in range(2):
                    for half in range(2):
                        lanes = slice(half * LANES, (half + 1) * LANES)
                        value = rows_ref[b, p, at // LANES + half, picked] * flags[c]
                        out = value * scale[top : top + count_windows, lanes]
                        y_ref[
                            b * chunks + at // LANES + half,
                            pl.ds((c * 2 + p) * count_windows, count_windows),
                        ] = out.astype(jnp.bfloat16)


def fold(values):
    index = lax.broadcasted_iota(jnp.int32, values[0].shape, 0)
    shift = 1
    while len(values) > 1:
        even = lax.rem(index // shift, 2) == 0
        paired = []
        for n in range(0, len(values), 2):
            u, v = values[n], values[n + 1]
            moved = pltpu.roll(jnp.where(even, v, u), 8 - shift, 0)
            paired.append(jnp.where(even, u, v) + moved)
        values = paired
        shift *= 2
    return values[0]


def by_eight(values):
    total = values[0:8]
    for at in range(8, values.shape[0], 8):
        total = total + values[at : at + 8]
    return total


def cross_row(wide_ref, r, rows, cols, finish):
    per_row = wide_ref.shape[0] // rows

    @pl.loop(0, r + 1)
    def _(q):
        for h in range(cols):
            reals, imags = [], []
            for k in range(2):
                first = q * per_row + h * 2 + k
                re_a, im_a = wide_ref[first, 0], wide_ref[first, 1]
                for n in range(per_row):
                    second = r * per_row + n
                    re_j, im_j = wide_ref[second, 0], wide_ref[second, 1]
                    reals.append(by_eight(re_a * re_j + im_a * im_j))
                    imags.append(by_eight(im_a * re_j - re_a * im_j))
            finish(h, q, jnp.concatenate([fold(reals), fold(imags)], axis=0))


def main_kernel(
    rows, cols, raw_ref, flag_ref, got_ref, x_ref, spread, sent, held, wide_ref, total_ref, pairs,
    send_sem, recv_sem, own_sem, back_send, back_recv, back_own, in_sem,
):
    count = rows * cols
    windows = x_ref.shape[1]
    part_windows = windows // 2
    row, col = lax.axis_index("row"), lax.axis_index("col")
    me = row * cols + col
    order = sorted(range(1, count), key=lambda k: abs(k - count // 2))

    def place_of(peer):
        return {"row": peer // cols, "col": lax.rem(peer, cols)}

    barrier = pltpu.get_barrier_semaphore()
    loads = []
    for half in range(2):
        part = pl.ds(half * part_windows, part_windows)
        loads.append(
            pltpu.make_async_copy(raw_ref.at[:, part], x_ref.at[:, part], in_sem.at[half])
        )
        loads[half].start()
    for k in range(1, count):
        pl.semaphore_signal(
            barrier,
            inc=1,
            device_id=place_of(lax.rem(me + k, count)),
            device_id_type=pl.DeviceIdType.MESH,
        )
    copies, owns = [[], []], []
    for half in range(2):
        loads[half].wait()
        whiten_windows(x_ref, flag_ref, spread, sent.at[half], half * part_windows, part_windows)
        if half == 0:
            pl.semaphore_wait(barrier, count - 1)
        for k in order:
            peer = lax.rem(me + k, count)
            copy = pltpu.make_async_remote_copy(
                src_ref=sent.at[half, peer],
                dst_ref=held.at[half, me],
                send_sem=send_sem.at[half, k],
                recv_sem=recv_sem.at[half, k],
                device_id=place_of(peer),
                device_id_type=pl.DeviceIdType.MESH,
            )
            copy.start()
            copies[half].append(copy)
        own = pltpu.make_async_copy(sent.at[half, me], held.at[half, me], own_sem.at[half])
        own.start()
        owns.append(own)

    def widen(half):
        owns[half].wait()
        for copy in copies[half]:
            copy.wait_recv()

        @pl.loop(0, count)
        def _(n):
            for c in range(2):
                for p in range(2):
                    wide_ref[n * 2 + c, p] = held[
                        half, n, pl.ds((c * 2 + p) * part_windows, part_windows)
                    ].astype(jnp.float32)

    widen(0)

    @pl.loop(0, rows)
    def _(r):
        def keep(h, q, value):
            total_ref[r * cols + h, q] = value

        cross_row(wide_ref, r, rows, cols, keep)

    widen(1)

    def back_copy(k, h):
        to = k * cols + h
        return pltpu.make_async_remote_copy(
            src_ref=pairs.at[to, pl.ds(0, k + 1)],
            dst_ref=got_ref.at[me, pl.ds(0, k + 1)],
            send_sem=back_send.at[to],
            recv_sem=back_recv.at[me],
            device_id={"row": k, "col": h},
            device_id_type=pl.DeviceIdType.MESH,
        )

    def own_copy(k, h):
        to = k * cols + h
        return pltpu.make_async_copy(
            pairs.at[to, pl.ds(0, k + 1)], got_ref.at[to, pl.ds(0, k + 1)], back_own
        )

    @pl.loop(0, rows)
    def _(step):
        r = lax.rem(row + rows // 2 + step, rows)

        def keep(h, q, value):
            pairs[r * cols + h, q] = (total_ref[r * cols + h, q] + value).astype(jnp.bfloat16)

        cross_row(wide_ref, r, rows, cols, keep)
        for k in range(rows):

            @pl.when(r == k)
            def _():
                for h in range(cols):

                    @pl.when(me != k * cols + h)
                    def _():
                        back_copy(k, h).start()

                    @pl.when(me == k * cols + h)
                    def _():
                        own_copy(k, h).start()

    for half in range(2):
        for copy in copies[half]:
            copy.wait_send()
    for k in range(rows):
        for h in range(cols):

            @pl.when(me != k * cols + h)
            def _():
                back_copy(k, h).wait_send()

    for k in range(rows):

        @pl.when(row == k)
        def _():
            for n in range(count):

                @pl.when(me != n)
                def _():
                    pltpu.make_async_remote_copy(
                        src_ref=pairs.at[0, pl.ds(0, k + 1)],
                        dst_ref=got_ref.at[n, pl.ds(0, k + 1)],
                        send_sem=back_send.at[n],
                        recv_sem=back_recv.at[n],
                        device_id={"row": n // cols, "col": n % cols},
                        device_id_type=pl.DeviceIdType.MESH,
                    ).wait_recv()

                @pl.when(me == n)
                def _():
                    own_copy(k, n % cols).wait()


def place_kernel(bands, x_ref, o_ref, taken, placed, in_sem, out_sem):
    row, col = lax.axis_index("row"), lax.axis_index("col")
    chunks, rows = x_ref.shape[0] // bands, x_ref.shape[1]
    loads = []
    for b in range(bands):
        here = pl.ds(b * chunks, chunks)
        loads.append(pltpu.make_async_copy(x_ref.at[here], taken.at[here], in_sem.at[b]))
        loads[-1].start()
    index = lax.broadcasted_iota(jnp.int32, (8, LANES), 0)
    second = row * 4 + lax.rem(index, 4)
    stores = []
    for b in range(bands):
        loads[b].wait()
        for p in range(2):
            for q in range(rows):
                keep = q * 4 + col * 2 + index // 4 <= second
                for c in range(chunks):
                    pair = taken[b * chunks + c, q].astype(jnp.float32)
                    value = jnp.where(keep, pair[p * 8 : p * 8 + 8], 0.0)
                    for k in range(2):
                        placed[b, p, 0, q * 2 + k, :, c * LANES : (c + 1) * LANES] = value[
                            k * 4 : k * 4 + 4
                        ]
            stores.append(
                pltpu.make_async_copy(placed.at[b, p], o_ref.at[b, p], out_sem.at[b, p])
            )
            stores[-1].start()
    for store in stores:
        store.wait()


def exchange_form(rows, cols, spectra, window_flags):
    bands, windows, parts, chans, bins = spectra.shape
    count = rows * cols
    height = chans * parts * windows
    got = pl.pallas_call(
        functools.partial(main_kernel, rows, cols),
        out_shape=jax.ShapeDtypeStruct((count, rows, 16, LANES), jnp.bfloat16),
        in_specs=[
            pl.BlockSpec(memory_space=pl.ANY),
            pl.BlockSpec(memory_space=pltpu.VMEM),
        ],
        out_specs=pl.BlockSpec(memory_space=pl.ANY),
        scratch_shapes=[
            pltpu.VMEM(spectra.shape, spectra.dtype),
            pltpu.VMEM((bands, parts, bins // LANES, windows // 2 * chans, LANES), jnp.float32),
            pltpu.VMEM((2, count, height // 2, LANES), jnp.bfloat16),
            pltpu.VMEM((2, count, height // 2, LANES), jnp.bfloat16),
            pltpu.VMEM((count * chans, parts, windows // 2, LANES), jnp.float32),
            pltpu.VMEM((count, rows, 16, LANES), jnp.float32),
            pltpu.VMEM((count, rows, 16, LANES), jnp.bfloat16),
            pltpu.SemaphoreType.DMA((2, count)),
            pltpu.SemaphoreType.DMA((2, count)),
            pltpu.SemaphoreType.DMA((2,)),
            pltpu.SemaphoreType.DMA((count,)),
            pltpu.SemaphoreType.DMA((count,)),
            pltpu.SemaphoreType.DMA,
            pltpu.SemaphoreType.DMA((2,)),
        ],
        compiler_params=pltpu.CompilerParams(collective_id=0, has_side_effects=True),
    )(spectra, jnp.transpose(window_flags))
    shape = (bands, 2, 1, rows * chans, cols * chans, bins)
    return pl.pallas_call(
        functools.partial(place_kernel, bands),
        in_specs=[pl.BlockSpec(memory_space=pl.ANY)],
        out_specs=pl.BlockSpec(memory_space=pl.ANY),
        out_shape=jax.ShapeDtypeStruct(shape, jnp.float32),
        scratch_shapes=[
            pltpu.VMEM(got.shape, got.dtype),
            pltpu.VMEM(shape, jnp.float32),
            pltpu.SemaphoreType.DMA((bands,)),
            pltpu.SemaphoreType.DMA((bands, 2)),
        ],
    )(got)


def solution(mesh):
    rows, cols = mesh.shape["row"], mesh.shape["col"]

    def on_device(spectra, window_flags):
        bands, windows, _, chans, bins = spectra.shape
        fits = (
            bands * bins == rows * cols * LANES
            and bins % (2 * LANES) == 0
            and chans == 2
            and cols == 2
            and windows % 32 == 0
        )
        if fits:
            return exchange_form(rows, cols, spectra, window_flags)
        return gather_form(spectra, window_flags)

    in_specs = (P("parts", None, None, ("row", "col"), None), P("parts", ("row", "col")))
    out_specs = P("parts", None, "col", None, "row", None)
    return jax.shard_map(
        on_device, mesh=mesh, in_specs=in_specs, out_specs=out_specs, check_vma=False
    )
```

```python
import functools

import jax
import jax.numpy as jnp
from jax import lax
from jax.experimental import pallas as pl
from jax.experimental.pallas import tpu as pltpu
from jax.sharding import PartitionSpec as P

HALFWIN = 64
LANES = 128
epsilon = 1e-06


def window_mean(magnitude):
    bins = magnitude.shape[-1]
    lead = [(0, 0)] * (magnitude.ndim - 1)
    padded = jnp.pad(magnitude, lead + [(HALFWIN + 1, HALFWIN)])
    running = jnp.cumsum(padded, axis=-1)
    total = running[..., 2 * HALFWIN + 1 :] - running[..., :bins]
    positions = jnp.arange(bins, dtype=jnp.int32)
    counted = (
        jnp.minimum(positions + HALFWIN, bins - 1) - jnp.maximum(positions - HALFWIN, 0) + 1
    ).astype(jnp.float32)
    return total / counted


def whiten(values):
    magnitude = jnp.sqrt(values[:, :, 0] * values[:, :, 0] + values[:, :, 1] * values[:, :, 1])
    smooth = window_mean(magnitude)
    return (values / (smooth[:, :, None] + epsilon)).astype(jnp.bfloat16)


def combine_parts(prods, keep):
    real_part = prods[..., 0, 0, :, :, :] + prods[..., 1, 1, :, :, :]
    imag_part = prods[..., 1, 0, :, :, :] - prods[..., 0, 1, :, :, :]
    return jnp.stack([real_part * keep, imag_part * keep], axis=-4)


def gather_form(spectra, window_flags):
    per_device = spectra.shape[3]
    flag_values = window_flags.astype(jnp.float32)[None, :, None, :, None]
    payload = whiten(spectra.astype(jnp.float32) * flag_values)
    row_index = lax.axis_index("row")
    col_index = lax.axis_index("col")
    col_count = lax.axis_size("col")
    row_count = lax.axis_size("row")
    half_size = row_count * per_device
    cols_here = col_count * per_device
    slot = jnp.arange(half_size, dtype=jnp.int32)
    first = (slot // per_device * col_count + col_index) * per_device + slot % per_device
    second = row_index * cols_here + jnp.arange(cols_here, dtype=jnp.int32)
    keep = (first[:, None] <= second[None, :]).astype(jnp.float32)[:, :, None]
    pieces = []
    for band_index in range(spectra.shape[0]):
        first_rows = lax.all_gather(payload[band_index : band_index + 1], "row", axis=3, tiled=True)
        second_rows = lax.all_gather(
            payload[band_index : band_index + 1], "col", axis=3, tiled=True
        )
        prods = jnp.einsum(
            "wpif,wqjf->pqijf", first_rows[0], second_rows[0], preferred_element_type=jnp.float32
        )
        pieces.append(combine_parts(prods, keep))
    result = jnp.stack(pieces, axis=0)
    return result[:, :, None]


def spread_windows(x_ref, flag_ref, rows_ref, start_window, count_windows):
    bands, _, parts, chans, _ = x_ref.shape
    for b in range(bands):
        for w in range(count_windows):
            for p in range(parts):
                pair = x_ref[b, start_window + w, p].astype(jnp.float32)
                for n in range(rows_ref.shape[2]):
                    rows_ref[b, p, n, pl.ds(w * chans, chans)] = pair[:, n * LANES : (n + 1) * LANES]
    extent = (count_windows, flag_ref.shape[1])
    here = lax.broadcasted_iota(jnp.int32, extent, 0) + start_window
    same = here == lax.broadcasted_iota(jnp.int32, extent, 1)
    flags = flag_ref[...].astype(jnp.float32)
    return [
        jnp.sum(jnp.where(same, flags[c : c + 1], 0.0), axis=1, keepdims=True)
        for c in range(chans)
    ]


def whiten_windows(x_ref, flag_ref, rows_ref, y_ref, start_window, count_windows):
    bands, _, _, chans, bins = x_ref.shape
    flags = spread_windows(x_ref, flag_ref, rows_ref, start_window, count_windows)
    step = 2 * LANES
    chunks = bins // LANES
    near = lax.broadcasted_iota(jnp.int32, (2 * step, step), 0) - LANES
    here = lax.broadcasted_iota(jnp.int32, (2 * step, step), 1)
    inside = (jnp.abs(near - here) <= HALFWIN).astype(jnp.float32).astype(jnp.bfloat16)
    mags = []
    for b in range(bands):
        for c in range(chans):
            picked = pl.ds(c, count_windows, stride=chans)
            line = []
            for n in range(chunks):
                re = rows_ref[b, 0, n, picked] * flags[c]
                im = rows_ref[b, 1, n, picked] * flags[c]
                line.append(jnp.sqrt(re * re + im * im))
            mags.append(jnp.concatenate(line, axis=1))
    mag = jnp.concatenate(mags, axis=0)
    high = mag.astype(jnp.bfloat16)
    low = (mag - high.astype(jnp.float32)).astype(jnp.bfloat16)
    for at in range(0, bins, step):
        start, stop = max(at - LANES, 0), min(at + step + LANES, bins)
        near_rows = inside[start - at + LANES : stop - at + LANES]
        total = jnp.dot(
            high[:, start:stop], near_rows, preferred_element_type=jnp.float32
        ) + jnp.dot(low[:, start:stop], near_rows, preferred_element_type=jnp.float32)
        spot = at + lax.broadcasted_iota(jnp.int32, (1, step), 1)
        counted = (
            jnp.minimum(spot + HALFWIN, bins - 1) - jnp.maximum(spot - HALFWIN, 0) + 1
        ).astype(jnp.float32)
        scale = 1.0 / (total / counted + epsilon)
        for b in range(bands):
            for c in range(chans):
                top = (b * chans + c) * count_windows
                picked = pl.ds(c, count_windows, stride=chans)
                for p in range(2):
                    for half in range(2):
                        lanes = slice(half * LANES, (half + 1) * LANES)
                        value = rows_ref[b, p, at // LANES + half, picked] * flags[c]
                        out = value * scale[top : top + count_windows, lanes]
                        y_ref[
                            b * chunks + at // LANES + half,
                            pl.ds((c * 2 + p) * count_windows, count_windows),
                        ] = out.astype(jnp.bfloat16)


def fold(values):
    index = lax.broadcasted_iota(jnp.int32, values[0].shape, 0)
    shift = 1
    while len(values) > 1:
        even = lax.rem(index // shift, 2) == 0
        paired = []
        for n in range(0, len(values), 2):
            u, v = values[n], values[n + 1]
            moved = pltpu.roll(jnp.where(even, v, u), 8 - shift, 0)
            paired.append(jnp.where(even, u, v) + moved)
        values = paired
        shift *= 2
    return values[0]


def by_eight(values):
    total = values[0:8]
    for at in range(8, values.shape[0], 8):
        total = total + values[at : at + 8]
    return total


def cross_row(wide_ref, r, rows, cols, finish):
    per_row = wide_ref.shape[0] // rows

    @pl.loop(0, r + 1)
    def _(q):
        for h in range(cols):
            reals, imags = [], []
            for k in range(2):
                first = q * per_row + h * 2 + k
                re_a, im_a = wide_ref[first, 0], wide_ref[first, 1]
                for n in range(per_row):
                    second = r * per_row + n
                    re_j, im_j = wide_ref[second, 0], wide_ref[second, 1]
                    reals.append(by_eight(re_a * re_j + im_a * im_j))
                    imags.append(by_eight(im_a * re_j - re_a * im_j))
            finish(h, q, jnp.concatenate([fold(reals), fold(imags)], axis=0))


def main_kernel(
    rows, cols, raw_ref, flag_ref, got_ref, x_ref, spread, sent, held, wide_ref, total_ref, pairs,
    send_sem, recv_sem, own_sem, back_send, back_recv, back_own, in_sem,
):
    count = rows * cols
    windows = x_ref.shape[1]
    part_windows = windows // 2
    row, col = lax.axis_index("row"), lax.axis_index("col")
    me = row * cols + col
    order = sorted(range(1, count), key=lambda k: abs(k - count // 2))

    def place_of(peer):
        return {"row": peer // cols, "col": lax.rem(peer, cols)}

    barrier = pltpu.get_barrier_semaphore()
    loads = []
    for half in range(2):
        part = pl.ds(half * part_windows, part_windows)
        loads.append(
            pltpu.make_async_copy(raw_ref.at[:, part], x_ref.at[:, part], in_sem.at[half])
        )
        loads[half].start()
    for k in range(1, count):
        pl.semaphore_signal(
            barrier,
            inc=1,
            device_id=place_of(lax.rem(me + k, count)),
            device_id_type=pl.DeviceIdType.MESH,
        )
    copies, owns = [[], []], []
    for half in range(2):
        loads[half].wait()
        whiten_windows(x_ref, flag_ref, spread, sent.at[half], half * part_windows, part_windows)
        if half == 0:
            pl.semaphore_wait(barrier, count - 1)
        for k in order:
            peer = lax.rem(me + k, count)
            copy = pltpu.make_async_remote_copy(
                src_ref=sent.at[half, peer],
                dst_ref=held.at[half, me],
                send_sem=send_sem.at[half, k],
                recv_sem=recv_sem.at[half, k],
                device_id=place_of(peer),
                device_id_type=pl.DeviceIdType.MESH,
            )
            copy.start()
            copies[half].append(copy)
        own = pltpu.make_async_copy(sent.at[half, me], held.at[half, me], own_sem.at[half])
        own.start()
        owns.append(own)

    def widen(half):
        owns[half].wait()
        for copy in copies[half]:
            copy.wait_recv()

        @pl.loop(0, count)
        def _(n):
            for c in range(2):
                for p in range(2):
                    wide_ref[n * 2 + c, p] = held[
                        half, n, pl.ds((c * 2 + p) * part_windows, part_windows)
                    ].astype(jnp.float32)

    widen(0)

    @pl.loop(0, rows)
    def _(r):
        def keep(h, q, value):
            total_ref[r * cols + h, q] = value

        cross_row(wide_ref, r, rows, cols, keep)

    widen(1)

    def back_copy(k, h):
        to = k * cols + h
        return pltpu.make_async_remote_copy(
            src_ref=pairs.at[to, pl.ds(0, k + 1)],
            dst_ref=got_ref.at[me, pl.ds(0, k + 1)],
            send_sem=back_send.at[to],
            recv_sem=back_recv.at[me],
            device_id={"row": k, "col": h},
            device_id_type=pl.DeviceIdType.MESH,
        )

    def own_copy(k, h):
        to = k * cols + h
        return pltpu.make_async_copy(
            pairs.at[to, pl.ds(0, k + 1)], got_ref.at[to, pl.ds(0, k + 1)], back_own
        )

    @pl.loop(0, rows)
    def _(step):
        r = rows - 1 - step

        def keep(h, q, value):
            pairs[r * cols + h, q] = (total_ref[r * cols + h, q] + value).astype(jnp.bfloat16)

        cross_row(wide_ref, r, rows, cols, keep)
        for k in range(rows):

            @pl.when(r == k)
            def _():
                for h in range(cols):

                    @pl.when(me != k * cols + h)
                    def _():
                        back_copy(k, h).start()

                    @pl.when(me == k * cols + h)
                    def _():
                        own_copy(k, h).start()

    for half in range(2):
        for copy in copies[half]:
            copy.wait_send()
    for k in range(rows):
        for h in range(cols):

            @pl.when(me != k * cols + h)
            def _():
                back_copy(k, h).wait_send()

    for k in range(rows):

        @pl.when(row == k)
        def _():
            for n in range(count):

                @pl.when(me != n)
                def _():
                    pltpu.make_async_remote_copy(
                        src_ref=pairs.at[0, pl.ds(0, k + 1)],
                        dst_ref=got_ref.at[n, pl.ds(0, k + 1)],
                        send_sem=back_send.at[n],
                        recv_sem=back_recv.at[n],
                        device_id={"row": n // cols, "col": n % cols},
                        device_id_type=pl.DeviceIdType.MESH,
                    ).wait_recv()

                @pl.when(me == n)
                def _():
                    own_copy(k, n % cols).wait()


def place_kernel(bands, x_ref, o_ref, taken, placed, in_sem, out_sem):
    row, col = lax.axis_index("row"), lax.axis_index("col")
    chunks, rows = x_ref.shape[0] // bands, x_ref.shape[1]
    loads = []
    for b in range(bands):
        here = pl.ds(b * chunks, chunks)
        loads.append(pltpu.make_async_copy(x_ref.at[here], taken.at[here], in_sem.at[b]))
        loads[-1].start()
    index = lax.broadcasted_iota(jnp.int32, (8, LANES), 0)
    second = row * 4 + lax.rem(index, 4)
    stores = []
    for b in range(bands):
        loads[b].wait()
        for p in range(2):
            for q in range(rows):
                keep = q * 4 + col * 2 + index // 4 <= second
                for c in range(chunks):
                    pair = taken[b * chunks + c, q].astype(jnp.float32)
                    value = jnp.where(keep, pair[p * 8 : p * 8 + 8], 0.0)
                    for k in range(2):
                        placed[b, p, 0, q * 2 + k, :, c * LANES : (c + 1) * LANES] = value[
                            k * 4 : k * 4 + 4
                        ]
            stores.append(
                pltpu.make_async_copy(placed.at[b, p], o_ref.at[b, p], out_sem.at[b, p])
            )
            stores[-1].start()
    for store in stores:
        store.wait()


def exchange_form(rows, cols, spectra, window_flags):
    bands, windows, parts, chans, bins = spectra.shape
    count = rows * cols
    height = chans * parts * windows
    got = pl.pallas_call(
        functools.partial(main_kernel, rows, cols),
        out_shape=jax.ShapeDtypeStruct((count, rows, 16, LANES), jnp.bfloat16),
        in_specs=[
            pl.BlockSpec(memory_space=pl.ANY),
            pl.BlockSpec(memory_space=pltpu.VMEM),
        ],
        out_specs=pl.BlockSpec(memory_space=pl.ANY),
        scratch_shapes=[
            pltpu.VMEM(spectra.shape, spectra.dtype),
            pltpu.VMEM((bands, parts, bins // LANES, windows // 2 * chans, LANES), jnp.float32),
            pltpu.VMEM((2, count, height // 2, LANES), jnp.bfloat16),
            pltpu.VMEM((2, count, height // 2, LANES), jnp.bfloat16),
            pltpu.VMEM((count * chans, parts, windows // 2, LANES), jnp.float32),
            pltpu.VMEM((count, rows, 16, LANES), jnp.float32),
            pltpu.VMEM((count, rows, 16, LANES), jnp.bfloat16),
            pltpu.SemaphoreType.DMA((2, count)),
            pltpu.SemaphoreType.DMA((2, count)),
            pltpu.SemaphoreType.DMA((2,)),
            pltpu.SemaphoreType.DMA((count,)),
            pltpu.SemaphoreType.DMA((count,)),
            pltpu.SemaphoreType.DMA,
            pltpu.SemaphoreType.DMA((2,)),
        ],
        compiler_params=pltpu.CompilerParams(collective_id=0, has_side_effects=True),
    )(spectra, jnp.transpose(window_flags))
    shape = (bands, 2, 1, rows * chans, cols * chans, bins)
    return pl.pallas_call(
        functools.partial(place_kernel, bands),
        in_specs=[pl.BlockSpec(memory_space=pl.ANY)],
        out_specs=pl.BlockSpec(memory_space=pl.ANY),
        out_shape=jax.ShapeDtypeStruct(shape, jnp.float32),
        scratch_shapes=[
            pltpu.VMEM(got.shape, got.dtype),
            pltpu.VMEM(shape, jnp.float32),
            pltpu.SemaphoreType.DMA((bands,)),
            pltpu.SemaphoreType.DMA((bands, 2)),
        ],
    )(got)


def solution(mesh):
    rows, cols = mesh.shape["row"], mesh.shape["col"]

    def on_device(spectra, window_flags):
        bands, windows, _, chans, bins = spectra.shape
        fits = (
            bands * bins == rows * cols * LANES
            and bins % (2 * LANES) == 0
            and chans == 2
            and cols == 2
            and windows % 32 == 0
        )
        if fits:
            return exchange_form(rows, cols, spectra, window_flags)
        return gather_form(spectra, window_flags)

    in_specs = (P("parts", None, None, ("row", "col"), None), P("parts", ("row", "col")))
    out_specs = P("parts", None, "col", None, "row", None)
    return jax.shard_map(
        on_device, mesh=mesh, in_specs=in_specs, out_specs=out_specs, check_vma=False
    )
```
